32 devices in a mesh: row: 4 (over z), col: 8 (over y, x, core).
Axes of the slice: x: 2, y: 2, z: 4, core: 2. Of those that a mesh axis runs over, the one named last changes fastest.
Arguments:
- parent_rhs: bfloat16 [12288, 128], P('row'), may hold values from -6 to 6
- parent_inverse: bfloat16 [48, 256, 256], P('row')
- parent_left: bfloat16 [48, 48, 128, 256], P('row', 'col'), may hold values from -0.0546875 to 0.0546875
- parent_right: bfloat16 [48, 48, 128, 256], P('row', 'col'), may hold values from -0.375 to 0.375
- parent_ranks: int32 [48, 48], P('row', 'col'), may hold values from 1 to 128, as said below
- parent_slots: int32 [48], P('col'), may hold values from 0 to 47, each once
- inner_left: bfloat16 [8, 15, 128, 256], P('row'), may hold values from -0.0546875 to 0.0546875
- inner_right: bfloat16 [8, 15, 128, 256], P('row'), may hold values from -0.375 to 0.375
- inner_ranks: int32 [8, 15], P('row'), may hold values from 1 to 128
- child_rhs: bfloat16 [8192, 128], P('row'), may hold values from -6 to 6
- child_inverse: bfloat16 [32, 256, 256], P('row')
- child_left: bfloat16 [32, 16, 128, 256], P('row', 'col'), may hold values from -0.09375 to 0.09375
- child_right: bfloat16 [32, 16, 128, 256], P('row', 'col'), may hold values from -0.375 to 0.375
- child_ranks: int32 [32, 16], P('row', 'col'), may hold values from 1 to 128
- child_slots: int32 [2, 16], P(None, 'col'), may hold values from 0 to 15, each once within a row
- child_inner_left: bfloat16 [8, 6, 128, 256], P('row'), may hold values from -0.09375 to 0.09375
- child_inner_right: bfloat16 [8, 6, 128, 256], P('row'), may hold values from -0.375 to 0.375
- child_inner_ranks: int32 [8, 6], P('row'), may hold values from 1 to 128
- border_left: bfloat16 [32, 16, 128, 256], P('row', 'col'), may hold values from -0.1875 to 0.1875
- border_right: bfloat16 [32, 16, 128, 256], P('row', 'col'), may hold values from -0.375 to 0.375
- border_ranks: int32 [32, 16], P('row', 'col'), may hold values from 1 to 128
- border_map: int32 [32], P('row'), may hold values from 0 to 47, as said below
Outputs:
- child_solution: bfloat16 [8192, 128], P('row')
- parent_solution: bfloat16 [12288, 128], P('row')
The draws below stay inside these ranges and needn't reach their ends.
Inputs may be any that keep to these rules, and one draw needn't show every extreme that they name: `parent_ranks`: only the leading rows of a tile's factors up to its rank are used. `border_map`: within one child's 16 border rows no parent tile row repeats; the two children may share parent tile rows. `parent_slots`: each tile column appears in exactly one slot. `child_slots`: for each child, each tile column appears in exactly one slot.
All inputs are finite; a program needn't handle non-finite values.
Results may differ from the reference program's by a relative error of at most 0.018.
Values may be sent and summed in bfloat16 or wider, within the bound.
A program may use at most 128 MiB of HBM per device.

```python
import math
import jax
import jax.numpy as jnp
from jax import lax

TILE = 256
RMAX = 128
NRHS = 128
PT = 48
CPIV = 16
CCON = 16
GP = 6
GC = 4
NSBP = 8
NSBC = 4
NPAIRP = 15
NPAIRC = 6
N_COL = 8


def rank_table(key, shape):
    values = jax.random.randint(key, shape, 1, RMAX + 1)
    flat = values.reshape(-1)
    flat = flat.at[0].set(RMAX)
    flat = flat.at[flat.shape[0] - 1].set(1)
    return flat.reshape(shape).astype(jnp.int32)


def inverse_table(key, count):
    noise = jax.random.normal(jax.random.fold_in(key, 1), (count, TILE, TILE), jnp.float32)
    diagonal = jax.random.uniform(jax.random.fold_in(key, 2), (count, TILE), jnp.float32, 0.7, 1.3)
    lower = jnp.tril(noise, -1) * (0.6 / math.sqrt(TILE))
    eye_table = jnp.eye(TILE, dtype=jnp.float32)[None, :, :]
    return (lower + eye_table * diagonal[:, :, None]).astype(jnp.bfloat16)


def draw_parent_inverse(key, part):
    return inverse_table(jax.random.fold_in(key, 101), PT)


def draw_child_inverse(key, part):
    return inverse_table(jax.random.fold_in(key, 102), 2 * CPIV)


def draw_parent_ranks(key, part):
    return rank_table(jax.random.fold_in(key, 11), (PT, PT))


def draw_inner_ranks(key, part):
    return rank_table(jax.random.fold_in(key, 12), (NSBP, NPAIRP))


def draw_child_ranks(key, part):
    return rank_table(jax.random.fold_in(key, 13), (2 * CPIV, CPIV))


def draw_child_inner_ranks(key, part):
    return rank_table(jax.random.fold_in(key, 14), (2 * NSBC, NPAIRC))


def draw_border_ranks(key, part):
    return rank_table(jax.random.fold_in(key, 15), (2 * CCON, CPIV))


def draw_border_map(key, part):
    pieces = []
    for child_index in range(2):
        subkey = jax.random.fold_in(key, 31 + child_index)
        inside = jax.random.permutation(jax.random.fold_in(subkey, 1), PT - 2).astype(jnp.int32) + 1
        chosen = jnp.concatenate([jnp.array([0, PT - 1], jnp.int32), inside[:CCON - 2]])
        order = jax.random.permutation(jax.random.fold_in(subkey, 2), CCON)
        pieces.append(chosen[order])
    return jnp.concatenate(pieces).astype(jnp.int32)


def levels(stream_key, dims, cuts, low, high):
    def one(dim, blocks):
        heights = jax.random.uniform(jax.random.fold_in(jax.random.fold_in(stream_key, 6), dim), (blocks,), jnp.float32, low / len(cuts), high / len(cuts))
        return jnp.repeat(jnp.exp(heights), dims[dim] // blocks).reshape((-1,) + (1,) * (len(dims) - dim - 1))

    gain = one(*cuts[0])
    for cut in cuts[1:]:
        gain = gain * one(*cut)
    return gain


def bell_draw(own_key, shape, width, bound, cuts=(), held_as=jnp.bfloat16):
    gain = levels(own_key, shape, cuts, -0.22, 0.18) if cuts else 1.0
    result = jax.random.normal(own_key, shape, jnp.float32) * width * gain
    return jnp.minimum(jnp.maximum(result, -bound), bound).astype(held_as)


def setup_inputs(seed: int = 0) -> dict:
    key_of = jax.random.split(jax.random.key(seed), 23)
    return {
        "parent_rhs": bell_draw(key_of[0], (PT * TILE, NRHS), 1.0, 6.0, ((0, 4),)),
        "parent_inverse": draw_parent_inverse(jax.random.fold_in(key_of[22], 71), 0),
        "parent_left": bell_draw(key_of[2], (PT, PT, RMAX, TILE), (2 * RMAX * PT) ** -0.5, 0.0546875, ((0, 4), (1, 8))),
        "parent_right": bell_draw(key_of[3], (PT, PT, RMAX, TILE), TILE ** -0.5, 0.375, ((0, 4), (1, 8))),
        "parent_ranks": draw_parent_ranks(jax.random.fold_in(key_of[22], 71), 0),
        "parent_slots": jax.random.permutation(key_of[5], PT).astype(jnp.int32),
        "inner_left": bell_draw(key_of[6], (NSBP, NPAIRP, RMAX, TILE), (2 * RMAX * PT) ** -0.5, 0.0546875, ((0, 4),)),
        "inner_right": bell_draw(key_of[7], (NSBP, NPAIRP, RMAX, TILE), TILE ** -0.5, 0.375, ((0, 4),)),
        "inner_ranks": draw_inner_ranks(jax.random.fold_in(key_of[22], 71), 0),
        "child_rhs": bell_draw(key_of[9], (2 * CPIV * TILE, NRHS), 1.0, 6.0, ((0, 4),)),
        "child_inverse": draw_child_inverse(jax.random.fold_in(key_of[22], 71), 0),
        "child_left": bell_draw(key_of[11], (2 * CPIV, CPIV, RMAX, TILE), (2 * RMAX * CPIV) ** -0.5, 0.09375, ((0, 4), (1, 8))),
        "child_right": bell_draw(key_of[12], (2 * CPIV, CPIV, RMAX, TILE), TILE ** -0.5, 0.375, ((0, 4), (1, 8))),
        "child_ranks": draw_child_ranks(jax.random.fold_in(key_of[22], 71), 0),
        "child_slots": jax.vmap(lambda own: jax.random.permutation(own, CPIV))(jax.random.split(key_of[14], 2)).reshape((2, CPIV)).astype(jnp.int32),
        "child_inner_left": bell_draw(key_of[15], (2 * NSBC, NPAIRC, RMAX, TILE), (2 * RMAX * CPIV) ** -0.5, 0.09375, ((0, 4),)),
        "child_inner_right": bell_draw(key_of[16], (2 * NSBC, NPAIRC, RMAX, TILE), TILE ** -0.5, 0.375, ((0, 4),)),
        "child_inner_ranks": draw_child_inner_ranks(jax.random.fold_in(key_of[22], 71), 0),
        "border_left": bell_draw(key_of[18], (2 * CCON, CPIV, RMAX, TILE), (RMAX * CPIV // 2) ** -0.5, 0.1875, ((0, 4), (1, 8))),
        "border_right": bell_draw(key_of[19], (2 * CCON, CPIV, RMAX, TILE), TILE ** -0.5, 0.375, ((0, 4), (1, 8))),
        "border_ranks": draw_border_ranks(jax.random.fold_in(key_of[22], 71), 0),
        "border_map": draw_border_map(jax.random.fold_in(key_of[22], 71), 0),
    }


def rounded(values):
    return lax.optimization_barrier(values.astype(jnp.bfloat16)).astype(jnp.float32)


def chain_block(right_side, far_part, inverse, near_left, near_right, near_ranks, group_size):
    rank_iota = jnp.arange(near_left.shape[1])
    solved = []
    for position in range(group_size):
        running_sum = right_side[position] - far_part[position]
        if position > 0:
            first_pair = position * (position - 1) // 2
            earlier = jnp.stack(solved).astype(jnp.float32)
            left_part = near_left[first_pair:first_pair + position].astype(jnp.float32)
            right_part = near_right[first_pair:first_pair + position].astype(jnp.float32)
            ranks_part = near_ranks[first_pair:first_pair + position]
            coeffs = jnp.einsum('mrt,mtn->mrn', right_part, earlier)
            keep_mask = (rank_iota[None, :] < ranks_part[:, None])[:, :, None]
            coeffs = rounded(jnp.where(keep_mask, coeffs, 0.0))
            running_sum = running_sum - jnp.einsum('mrt,mrn->tn', left_part, coeffs)
        residue = running_sum.astype(jnp.bfloat16)
        solved.append(jnp.dot(inverse[position], residue, preferred_element_type=jnp.float32).astype(jnp.bfloat16))
    return jnp.stack(solved)


def solve_front(right_side, inverse, left_factor, right_factor, tile_ranks, slots, near_left, near_right, near_ranks, group_size, owners):
    tile_count = inverse.shape[0]
    slot_count = left_factor.shape[1]
    tile_size = inverse.shape[1]
    columns = right_side.shape[2]
    rank_max = left_factor.shape[2]
    per_owner = slot_count // owners
    block_count = tile_count // group_size
    block_of = slots // group_size
    rank_iota = jnp.arange(rank_max)
    solution = jnp.zeros((tile_count, tile_size, columns), jnp.bfloat16)
    for block_index in range(block_count):
        lower = block_index * group_size
        upper = lower + group_size
        known_tiles = solution[slots].astype(jnp.float32)
        coeffs = jnp.einsum('gkrt,ktn->gkrn', right_factor[lower:upper].astype(jnp.float32), known_tiles)
        keep_mask = (rank_iota[None, None, :] < tile_ranks[lower:upper][:, :, None]) & (block_of < block_index)[None, :, None]
        coeffs = rounded(jnp.where(keep_mask[..., None], coeffs, 0.0))
        left_groups = left_factor[lower:upper].astype(jnp.float32).reshape(group_size, owners, per_owner, rank_max, tile_size)
        coeff_groups = coeffs.reshape(group_size, owners, per_owner, rank_max, columns)
        grouped = jnp.einsum('gcart,gcarn->gctn', left_groups, coeff_groups)
        far_part = jnp.sum(rounded(grouped), axis=1)
        new_tiles = chain_block(right_side[lower:upper], far_part, inverse[lower:upper], near_left[block_index], near_right[block_index], near_ranks[block_index], group_size)
        solution = solution.at[lower:upper].set(new_tiles)
    return solution


def reference(parent_rhs, parent_inverse, parent_left, parent_right, parent_ranks, parent_slots, inner_left, inner_right, inner_ranks, child_rhs, child_inverse, child_left, child_right, child_ranks, child_slots, child_inner_left, child_inner_right, child_inner_ranks, border_left, border_right, border_ranks, border_map):
    tile_size = parent_inverse.shape[1]
    columns = parent_rhs.shape[1]
    rank_iota = jnp.arange(parent_left.shape[2])
    extension = jnp.zeros((PT, tile_size, columns), jnp.float32)
    child_parts = []
    for child_index in range(2):
        lower = child_index * CPIV
        upper = lower + CPIV
        right_side = child_rhs[lower * tile_size:upper * tile_size].reshape(CPIV, tile_size, columns).astype(jnp.float32)
        solved = solve_front(right_side, child_inverse[lower:upper], child_left[lower:upper], child_right[lower:upper], child_ranks[lower:upper], child_slots[child_index], child_inner_left[child_index * NSBC:(child_index + 1) * NSBC], child_inner_right[child_index * NSBC:(child_index + 1) * NSBC], child_inner_ranks[child_index * NSBC:(child_index + 1) * NSBC], GC, N_COL)
        child_parts.append(solved)
        known_tiles = solved[child_slots[child_index]].astype(jnp.float32)
        border_low = child_index * CCON
        border_high = border_low + CCON
        coeffs = jnp.einsum('kjrt,jtn->kjrn', border_right[border_low:border_high].astype(jnp.float32), known_tiles)
        keep_mask = rank_iota[None, None, :] < border_ranks[border_low:border_high][:, :, None]
        coeffs = rounded(jnp.where(keep_mask[..., None], coeffs, 0.0))
        border = -jnp.einsum('kjrt,kjrn->ktn', border_left[border_low:border_high].astype(jnp.float32), coeffs)
        extension = extension.at[border_map[border_low:border_high]].add(border)
    parent_side = parent_rhs.reshape(PT, tile_size, columns).astype(jnp.float32) + extension
    parent = solve_front(parent_side, parent_inverse, parent_left, parent_right, parent_ranks, parent_slots, inner_left, inner_right, inner_ranks, GP, N_COL)
    child_solution = jnp.concatenate(child_parts, axis=0).reshape(2 * CPIV * tile_size, columns)
    parent_solution = parent.reshape(PT * tile_size, columns)
    return (child_solution, parent_solution)
```

```python
import functools

import jax
import jax.numpy as jnp
from jax import lax
from jax.experimental import pallas as pl
from jax.experimental.pallas import tpu as pltpu
from jax.sharding import PartitionSpec as P

MESH = pl.DeviceIdType.MESH
BF16 = jnp.bfloat16
F32 = jnp.float32


def dot_nt(a, b):
    return lax.dot_general(a, b, (((1,), (1,)), ((), ())), preferred_element_type=F32)


def dot_nn(a, b):
    return jnp.dot(a, b, preferred_element_type=F32)


def keep(coeffs, rank):
    lane = lax.broadcasted_iota(jnp.int32, coeffs.shape, 1)
    return jnp.where(lane < rank, coeffs, 0.0).astype(BF16)


def kernel(
    rows,
    cols,
    p_ranks, p_slots, in_ranks, c_ranks, c_slots, cin_ranks, b_ranks, b_inv,
    p_rhs, c_rhs,
    h_pinv, h_pl, h_pr, h_il, h_ir, h_cinv, h_cl, h_cr, h_cil, h_cir, h_bl, h_br,
    c_out, p_out,
    v_pinv, v_pl, v_pr, v_il, v_ir, v_cinv, v_cl, v_cr, v_cil, v_cir, v_bl, v_br,
    cx, px,
    cs, cf, ps, pf, bs, bf, bsum, zs, zf, side, acc,
    load_sem,
    cf_send, cf_recv, pf_send, pf_recv, bf_send, bf_recv, zf_send, zf_recv,
    cx_send, cx_recv, px_send, px_recv, cz_send, cz_recv, pz_send, pz_recv,
):
    row = lax.axis_index("row")
    col = lax.axis_index("col")
    half = rows // 2
    child = row // half
    place = row % half

    loads = [
        pltpu.make_async_copy(src, dst, load_sem.at[n])
        for n, (src, dst) in enumerate(
            (
                (h_cinv, v_cinv), (h_cir, v_cir), (h_cil, v_cil),
                (h_cr, v_cr), (h_cl, v_cl), (h_br, v_br), (h_bl, v_bl),
                (h_pinv, v_pinv), (h_ir, v_ir), (h_il, v_il),
                (h_pr, v_pr), (h_pl, v_pl),
            )
        )
    ]
    for load in loads:
        load.start()

    barrier = pltpu.get_barrier_semaphore()
    for d in range(1, cols):
        pl.semaphore_signal(
            barrier, inc=1, device_id=(row, lax.rem(col + d, cols)), device_id_type=MESH
        )
    for d in range(1, rows):
        pl.semaphore_signal(
            barrier, inc=1, device_id=(lax.rem(row + d, rows), col), device_id_type=MESH
        )
    pl.semaphore_wait(barrier, cols + rows - 2)

    def scatter_cols(sent, got, send_sem, recv_sem):
        copies = []
        for d in range(1, cols):
            peer = lax.rem(col + d, cols)
            copies.append(
                pltpu.make_async_remote_copy(
                    src_ref=sent.at[peer],
                    dst_ref=got.at[col],
                    send_sem=send_sem.at[d],
                    recv_sem=recv_sem.at[d],
                    device_id=(row, peer),
                    device_id_type=MESH,
                )
            )
        for copy in copies:
            copy.start()
        for copy in copies:
            copy.wait()

    def share_cols(x, first, count, send_sem, recv_sem):
        copies = []
        for d in range(1, cols):
            peer = lax.rem(col + d, cols)
            piece = x.at[pl.ds(first, count), col]
            copies.append(
                pltpu.make_async_remote_copy(
                    src_ref=piece,
                    dst_ref=piece,
                    send_sem=send_sem.at[d],
                    recv_sem=recv_sem.at[d],
                    device_id=(row, peer),
                    device_id_type=MESH,
                )
            )
        for copy in copies:
            copy.start()
        return copies

    def far_sums(x, first_row, group, limit, slots, ranks, v_r, v_l, out):
        nslots = v_r.shape[1]
        rmax, tile = v_r.shape[2], v_r.shape[3]
        for g in range(group):
            i = first_row + g
            parts = []
            for k in range(nslots):
                slot = slots(k)
                rank = ranks[i, k]
                if limit is not None:
                    rank = jnp.where(slot < limit, rank, 0)
                xk = x[slot].reshape(-1, tile)
                parts.append(keep(dot_nt(xk, v_r[i, k]), rank))
            coeffs = jnp.concatenate(parts, axis=1)
            total = dot_nn(coeffs, v_l[i].reshape(nslots * rmax, tile))
            out[:, g] = total.astype(BF16).reshape(cols, -1, tile)

    def chain(rhs, base, group, lb, v_inv, v_nr, v_nl, near_ranks, x, first):
        run = [acc[t] for t in range(group)]
        for t in range(group):
            y = dot_nt(run[t].astype(BF16), v_inv[base + t]).astype(BF16)
            x[first + t, col] = y
            for u in range(t + 1, group):
                p = u * (u - 1) // 2 + t
                coeffs = keep(dot_nt(y, v_nr[lb, p]), near_ranks[lb, p])
                run[u] = run[u] - dot_nn(coeffs, v_nl[lb, p])

    def solve(b, lb, group, x, rhs, slots, ranks, v_r, v_l, sent, got,
              send_sem, recv_sem, v_inv, v_nr, v_nl, near_ranks):
        base = lb * group
        first = b * group
        for g in range(group):
            acc[g] = rhs[base + g].astype(F32)

        @pl.when(b > 0)
        def _():
            far_sums(x, base, group, first, slots, ranks, v_r, v_l, sent.at[lb])
            scatter_cols(sent.at[lb], got.at[lb], send_sem, recv_sem.at[lb])
            for g in range(group):
                total = sent[lb, col, g].astype(F32)
                for d in range(1, cols):
                    total = total + got[lb, lax.rem(col + d, cols), g].astype(F32)
                acc[g] = acc[g] - total

        chain(rhs, base, group, lb, v_inv, v_nr, v_nl, near_ranks, x, first)

    c_blocks = v_cil.shape[0]
    c_group = v_cinv.shape[0] // c_blocks
    for load in loads[:5]:
        load.wait()

    @pl.loop(0, c_blocks * half)
    def _(b):
        owner = b // c_blocks
        lb = b % c_blocks
        first = b * c_group

        @pl.when(place == owner)
        def _():
            solve(b, lb, c_group, cx, c_rhs, lambda k: c_slots[child, k], c_ranks,
                  v_cr, v_cl, cs, cf, cf_send, cf_recv, v_cinv, v_cir, v_cil, cin_ranks)
            copies = []
            for d in range(1, half):
                peer = child * half + lax.rem(place + d, half)
                piece = cx.at[pl.ds(first, c_group), col]
                copies.append(
                    pltpu.make_async_remote_copy(
                        src_ref=piece, dst_ref=piece,
                        send_sem=cz_send.at[d], recv_sem=cz_recv.at[b],
                        device_id=(peer, col), device_id_type=MESH,
                    )
                )
            for copy in copies:
                copy.start()
            for copy in share_cols(cx, first, c_group, cx_send, cx_recv.at[b]):
                copy.wait()
            for copy in copies:
                copy.wait_send()

        @pl.when(place != owner)
        def _():
            piece = cx.at[pl.ds(first, c_group), col]
            pltpu.make_async_copy(piece, piece, cz_recv.at[b]).wait()
            for copy in share_cols(cx, first, c_group, cx_send, cx_recv.at[b]):
                copy.wait()

    for load in loads[5:7]:
        load.wait()
    n_border = v_bl.shape[0]
    far_sums(cx, 0, n_border, None, lambda k: c_slots[child, k], b_ranks, v_br, v_bl, bs)
    scatter_cols(bs, bf, bf_send, bf_recv)
    for k in range(n_border):
        total = bs[col, k].astype(F32)
        for d in range(1, cols):
            total = total + bf[lax.rem(col + d, cols), k].astype(F32)
        bsum[k] = total
    bsum[n_border] = jnp.zeros(bsum.shape[1:], F32)
    p_tiles = v_pinv.shape[0]
    copies = []
    for d in range(1, rows):
        peer = lax.rem(row + d, rows)
        for p in range(p_tiles):
            zs[d, p] = bsum[b_inv[peer * p_tiles + p]].astype(BF16)
        copies.append(
            pltpu.make_async_remote_copy(
                src_ref=zs.at[d], dst_ref=zf.at[d],
                send_sem=zf_send.at[d], recv_sem=zf_recv.at[d],
                device_id=(peer, col), device_id_type=MESH,
            )
        )
        copies[-1].start()
    c_tiles = v_cinv.shape[0]
    for t in range(c_tiles):
        c_out[t] = cx[place * c_tiles + t].reshape(c_out.shape[1:])
    for p in range(p_tiles):
        side[p] = p_rhs[p].astype(F32) - bsum[b_inv[row * p_tiles + p]]
    for copy in copies:
        copy.wait()
    for p in range(p_tiles):
        total = side[p]
        for d in range(1, rows):
            total = total - zf[d, p].astype(F32)
        side[p] = total

    p_blocks = v_il.shape[0]
    p_group = p_tiles // p_blocks
    for load in loads[7:]:
        load.wait()

    @pl.loop(0, p_blocks * rows)
    def _(b):
        owner = b // p_blocks
        lb = b % p_blocks
        first = b * p_group

        @pl.when(row == owner)
        def _():
            solve(b, lb, p_group, px, side, lambda k: p_slots[k], p_ranks,
                  v_pr, v_pl, ps, pf, pf_send, pf_recv, v_pinv, v_ir, v_il, in_ranks)
            piece = px.at[pl.ds(first, p_group), col]

            def below(d):
                return pltpu.make_async_remote_copy(
                    src_ref=piece, dst_ref=piece,
                    send_sem=pz_send.at[d], recv_sem=pz_recv.at[b],
                    device_id=(lax.rem(row + d, rows), col), device_id_type=MESH,
                )

            for d in range(1, rows):
                @pl.when(row + d < rows)
                def _():
                    below(d).start()
            for copy in share_cols(px, first, p_group, px_send, px_recv.at[b]):
                copy.wait()
            for d in range(1, rows):
                @pl.when(row + d < rows)
                def _():
                    below(d).wait_send()

        @pl.when(row > owner)
        def _():
            piece = px.at[pl.ds(first, p_group), col]
            pltpu.make_async_copy(piece, piece, pz_recv.at[b]).wait()
            for copy in share_cols(px, first, p_group, px_send, px_recv.at[b]):
                copy.wait()

    for t in range(p_tiles):
        p_out[t] = px[row * p_tiles + t].reshape(p_out.shape[1:])


def on_device(
    rows,
    cols,
    parent_rhs, parent_inverse, parent_left, parent_right, parent_ranks, parent_slots,
    inner_left, inner_right, inner_ranks,
    child_rhs, child_inverse, child_left, child_right, child_ranks, child_slots,
    child_inner_left, child_inner_right, child_inner_ranks,
    border_left, border_right, border_ranks, border_map,
):
    tile = parent_inverse.shape[1]
    nrhs = parent_rhs.shape[1]
    width = nrhs // cols
    col = lax.axis_index("col")
    p_tiles, c_tiles = parent_inverse.shape[0], child_inverse.shape[0]
    p_blocks, c_blocks = inner_left.shape[0], child_inner_left.shape[0]
    p_group, c_group = p_tiles // p_blocks, c_tiles // c_blocks
    n_border = border_left.shape[0]
    p_all = p_tiles * rows
    c_all = c_tiles * (rows // 2)

    def cut(rhs, tiles):
        mine = lax.dynamic_slice_in_dim(rhs, col * width, width, axis=1)
        return mine.reshape(tiles, tile, width).transpose(0, 2, 1)

    index = jnp.arange(n_border, dtype=jnp.int32)[:, None]
    hit = border_map[:, None] == jnp.arange(p_all, dtype=jnp.int32)[None, :]
    inverse_map = jnp.min(jnp.where(hit, index, n_border), axis=0)

    big = (
        parent_inverse, parent_left, parent_right, inner_left, inner_right,
        child_inverse, child_left, child_right, child_inner_left, child_inner_right,
        border_left, border_right,
    )
    smem = pl.BlockSpec(memory_space=pltpu.SMEM)
    vmem = pl.BlockSpec(memory_space=pltpu.VMEM)
    hbm = pl.BlockSpec(memory_space=pl.ANY)
    dma = pltpu.SemaphoreType.DMA
    c_out, p_out = pl.pallas_call(
        functools.partial(kernel, rows, cols),
        out_shape=(
            jax.ShapeDtypeStruct((c_tiles, nrhs, tile), BF16),
            jax.ShapeDtypeStruct((p_tiles, nrhs, tile), BF16),
        ),
        in_specs=[smem] * 8 + [vmem] * 2 + [hbm] * len(big),
        out_specs=(vmem, vmem),
        scratch_shapes=[pltpu.VMEM(a.shape, a.dtype) for a in big]
        + [
            pltpu.VMEM((c_all, cols, width, tile), BF16),
            pltpu.VMEM((p_all, cols, width, tile), BF16),
            pltpu.VMEM((c_blocks, cols, c_group, width, tile), BF16),
            pltpu.VMEM((c_blocks, cols, c_group, width, tile), BF16),
            pltpu.VMEM((p_blocks, cols, p_group, width, tile), BF16),
            pltpu.VMEM((p_blocks, cols, p_group, width, tile), BF16),
            pltpu.VMEM((cols, n_border, width, tile), BF16),
            pltpu.VMEM((cols, n_border, width, tile), BF16),
            pltpu.VMEM((n_border + 1, width, tile), F32),
            pltpu.VMEM((rows, p_tiles, width, tile), BF16),
            pltpu.VMEM((rows, p_tiles, width, tile), BF16),
            pltpu.VMEM((p_tiles, width, tile), F32),
            pltpu.VMEM((max(p_group, c_group), width, tile), F32),
            dma((len(big),)),
            dma((cols,)), dma((c_blocks, cols)),
            dma((cols,)), dma((p_blocks, cols)),
            dma((cols,)), dma((cols,)),
            dma((rows,)), dma((rows,)),
            dma((cols,)), dma((c_blocks * (rows // 2), cols)),
            dma((cols,)), dma((p_blocks * rows, cols)),
            dma((rows,)), dma((c_blocks * (rows // 2),)),
            dma((rows,)), dma((p_blocks * rows,)),
        ],
        compiler_params=pltpu.CompilerParams(
            collective_id=0, has_side_effects=True, vmem_limit_bytes=60 * 1024 * 1024
        ),
    )(
        parent_ranks, parent_slots, inner_ranks, child_ranks, child_slots,
        child_inner_ranks, border_ranks, inverse_map,
        cut(parent_rhs, p_tiles), cut(child_rhs, c_tiles),
        *big,
    )
    return (
        c_out.transpose(0, 2, 1).reshape(c_tiles * tile, nrhs),
        p_out.transpose(0, 2, 1).reshape(p_tiles * tile, nrhs),
    )


def solution(mesh):
    two, three, four = P("row", None), P("row", None, None), P("row", None, None, None)
    placed = (
        two, three, P("row", "col", None, None), P("row", "col", None, None),
        P("row", "col"), P("col"), four, four, two,
        two, three, P("row", "col", None, None), P("row", "col", None, None),
        P("row", "col"), P(None, "col"), four, four, two,
        P("row", "col", None, None), P("row", "col", None, None), P("row", "col"), P("row"),
    )
    return jax.shard_map(
        functools.partial(on_device, mesh.shape["row"], mesh.shape["col"]),
        mesh=mesh,
        in_specs=placed,
        out_specs=(two, two),
        check_vma=False,
    )
```

```python
import functools
import math

import jax
import jax.numpy as jnp
from jax import lax
from jax.experimental import pallas as pl
from jax.experimental.pallas import tpu as pltpu
from jax.sharding import PartitionSpec as P

MESH = pl.DeviceIdType.MESH
BF16 = jnp.bfloat16
F32 = jnp.float32


def dot_nt(a, b):
    return lax.dot_general(a, b, (((1,), (1,)), ((), ())), preferred_element_type=F32)


def dot_nn(a, b):
    return jnp.dot(a, b, preferred_element_type=F32)


def keep(coeffs, rank):
    lane = lax.broadcasted_iota(jnp.int32, coeffs.shape, 1)
    return jnp.where(lane < rank, coeffs, 0.0).astype(BF16)


class View:
    def __init__(self, table, start, shape):
        self.table, self.start, self.shape = table, start, shape

    def __getitem__(self, at):
        if len(self.shape) == 1:
            return self.table[self.start + at]
        return self.table[self.start + at[0] * self.shape[1] + at[1]]


def views(table, shapes):
    start, found = 0, []
    for shape in shapes:
        found.append(View(table, start, shape))
        start += math.prod(shape)
    return found


def kernel(
    rows,
    cols,
    shapes,
    table,
    p_side, c_side,
    h_pinv, h_pl, h_pr, h_il, h_ir, h_cinv, h_cl, h_cr, h_cil, h_cir, h_bl, h_br,
    c_out, p_out,
    v_pinv, v_pl, v_pr, v_il, v_ir, v_cinv, v_cl, v_cr, v_cil, v_cir, v_bl, v_br,
    cx, px,
    cs, cf, ps, pf, bs, bf, bsum, zs, zf, side, known, p_rhs, c_rhs,
    load_sem,
    cf_send, cf_recv, pf_send, pf_recv, bf_send, bf_recv, zf_send, zf_recv,
    cx_send, cx_recv, px_send, px_recv, cz_send, cz_recv, pz_send, pz_recv,
):
    row = lax.axis_index("row")
    col = lax.axis_index("col")
    p_ranks, p_slots, in_ranks, c_ranks, c_slots, cin_ranks, b_ranks, b_inv = views(table, shapes)
    half = rows // 2
    child = row // half
    place = row % half

    loads = [
        pltpu.make_async_copy(src, dst, load_sem.at[n])
        for n, (src, dst) in enumerate(
            (
                (h_cinv, v_cinv), (h_cir, v_cir), (h_cil, v_cil),
                (h_cr, v_cr), (h_cl, v_cl), (h_br, v_br), (h_bl, v_bl),
                (h_pinv, v_pinv), (h_ir, v_ir), (h_il, v_il),
                (h_pr, v_pr), (h_pl, v_pl),
            )
        )
    ]
    for load in loads:
        load.start()

    barrier = pltpu.get_barrier_semaphore()
    for d in range(1, cols):
        pl.semaphore_signal(
            barrier, inc=1, device_id=(row, lax.rem(col + d, cols)), device_id_type=MESH
        )
    for d in range(1, rows):
        pl.semaphore_signal(
            barrier, inc=1, device_id=(lax.rem(row + d, rows), col), device_id_type=MESH
        )
    pl.semaphore_wait(barrier, cols + rows - 2)

    tile = c_side.shape[0] // v_cinv.shape[0]
    for side_in, turned in ((c_side, c_rhs), (p_side, p_rhs)):
        for n in range(turned.shape[0]):
            turned[n] = side_in[n * tile:(n + 1) * tile].T.reshape(turned.shape[1:])

    def scatter_tile(sent, got, g, send_sem, recv_sem):
        copies = []
        for d in range(1, cols):
            peer = lax.rem(col + d, cols)
            copies.append(
                pltpu.make_async_remote_copy(
                    src_ref=sent.at[peer, g],
                    dst_ref=got.at[col, g],
                    send_sem=send_sem.at[g, d],
                    recv_sem=recv_sem.at[g, d],
                    device_id=(row, peer),
                    device_id_type=MESH,
                )
            )
        return copies

    def gathered(sent, got, g):
        total = sent[col, g].astype(F32)
        for d in range(1, cols):
            total = total + got[lax.rem(col + d, cols), g].astype(F32)
        return total

    def share_cols(piece, send_sem, recv_sem):
        copies = []
        for d in range(1, cols):
            copies.append(
                pltpu.make_async_remote_copy(
                    src_ref=piece,
                    dst_ref=piece,
                    send_sem=send_sem.at[d],
                    recv_sem=recv_sem.at[d],
                    device_id=(row, lax.rem(col + d, cols)),
                    device_id_type=MESH,
                )
            )
        return copies

    def far_sums(x, first_row, group, limit, slots, ranks, v_r, v_l, sent, got, send_sem, recv_sem):
        nslots = v_r.shape[1]
        rmax, tile = v_r.shape[2], v_r.shape[3]
        for k in range(nslots):
            known[k] = x[slots(k)].reshape(known.shape[1:])
        for g in range(group):
            i = first_row + g
            parts = []
            for k in range(nslots):
                rank = ranks[i, k]
                if limit is not None:
                    rank = jnp.where(slots(k) < limit, rank, 0)
                parts.append(keep(dot_nt(known[k], v_r[i, k]), rank))
            coeffs = jnp.concatenate(parts, axis=1)
            total = dot_nn(coeffs, v_l[i].reshape(nslots * rmax, tile))
            sent[:, g] = total.astype(BF16).reshape(cols, -1, tile)
            for copy in scatter_tile(sent, got, g, send_sem, recv_sem):
                copy.start()

    def solve(b, lb, group, x, rhs, slots, ranks, v_r, v_l, sent, got,
              send_sem, recv_sem, v_inv, v_nr, v_nl, near_ranks, after, far):
        base = lb * group
        first = b * group
        if far:
            far_sums(x, base, group, first, slots, ranks, v_r, v_l,
                     sent.at[lb], got.at[lb], send_sem, recv_sem.at[lb])
        near = [None] * group
        for t in range(group):
            residue = rhs(base + t).astype(F32)
            if near[t] is not None:
                residue = residue - near[t]
            if far:
                for copy in scatter_tile(sent.at[lb], got.at[lb], t, send_sem, recv_sem.at[lb]):
                    copy.wait()
                residue = residue - gathered(sent.at[lb], got.at[lb], t)
            y = dot_nt(residue.astype(BF16), v_inv[base + t]).astype(BF16)
            x[first + t, col] = y
            after(first + t)
            for u in range(t + 1, group):
                p = u * (u - 1) // 2 + t
                coeffs = keep(dot_nt(y, v_nr[lb, p]), near_ranks[lb, p])
                part = dot_nn(coeffs, v_nl[lb, p])
                near[u] = part if near[u] is None else near[u] + part

    def front(steps, blocks, group, place, peers, reaches, x, z_send, z_recv, x_send, x_recv, solver):
        def step(b, far):
            owner = b // blocks
            lb = b % blocks
            first = b * group
            whole = x.at[pl.ds(first, group), col]

            def across(piece, t, d):
                return pltpu.make_async_remote_copy(
                    src_ref=piece, dst_ref=piece,
                    send_sem=z_send.at[d], recv_sem=z_recv.at[b, t],
                    device_id=(peers(d), col), device_id_type=MESH,
                )

            def each_peer(act):
                for d in range(1, steps // blocks):
                    pl.when(reaches(d))(functools.partial(act, d))

            @pl.when(place == owner)
            def _():
                def after(tile):
                    piece = x.at[tile, col]
                    each_peer(lambda d: across(piece, tile - first, d).start())
                    for copy in share_cols(piece, x_send, x_recv.at[b]):
                        copy.start()

                solver(b, lb, after, far)
                for copy in share_cols(whole, x_send, x_recv.at[b]):
                    copy.wait()
                each_peer(lambda d: across(whole, 0, d).wait_send())

            @pl.when(takes(owner))
            def _():
                for t in range(group):
                    piece = x.at[first + t, col]
                    pltpu.make_async_copy(piece, piece, z_recv.at[b, t]).wait()
                    for copy in share_cols(piece, x_send, x_recv.at[b]):
                        copy.start()
                for copy in share_cols(whole, x_send, x_recv.at[b]):
                    copy.wait()

        if reaches is always:
            takes = lambda owner: place != owner
        else:
            takes = lambda owner: place > owner
        step(0, False)
        pl.loop(1, steps)(lambda b: step(b, True))

    always = lambda d: d > 0

    c_blocks = v_cil.shape[0]
    c_group = v_cinv.shape[0] // c_blocks
    for load in loads[:5]:
        load.wait()

    def child_solver(b, lb, after, far):
        solve(b, lb, c_group, cx, lambda n: c_rhs[n, col], lambda k: c_slots[child, k], c_ranks, v_cr, v_cl,
              cs, cf, cf_send, cf_recv, v_cinv, v_cir, v_cil, cin_ranks, after, far)

    front(c_blocks * half, c_blocks, c_group, place,
          lambda d: child * half + lax.rem(place + d, half), always,
          cx, cz_send, cz_recv, cx_send, cx_recv, child_solver)

    for load in loads[5:7]:
        load.wait()
    n_border = v_bl.shape[0]
    far_sums(cx, 0, n_border, None, lambda k: c_slots[child, k], b_ranks, v_br, v_bl,
             bs, bf, bf_send, bf_recv)
    for k in range(n_border):
        for copy in scatter_tile(bs, bf, k, bf_send, bf_recv):
            copy.wait()
        bsum[k] = gathered(bs, bf, k)
    bsum[n_border] = jnp.zeros(bsum.shape[1:], F32)
    p_tiles = v_pinv.shape[0]
    p_blocks = v_il.shape[0]
    p_group = p_tiles // p_blocks

    def lifted(q, l):
        return pltpu.make_async_remote_copy(
            src_ref=zs.at[q, l], dst_ref=zf.at[row, l],
            send_sem=zf_send.at[q, l], recv_sem=zf_recv.at[row, l],
            device_id=(q, col), device_id_type=MESH,
        )

    for q in range(rows):
        @pl.when(row != q)
        def _():
            for l in range(p_blocks):
                for g in range(p_group):
                    p = (q * p_blocks + l) * p_group + g
                    zs[q, l, g] = bsum[b_inv[p]].astype(BF16)
                lifted(q, l).start()

    for p in range(p_tiles):
        side[p] = p_rhs[p, col].astype(F32) - bsum[b_inv[row * p_tiles + p]]
    c_tiles = v_cinv.shape[0]
    for t in range(c_tiles):
        c_out[t] = cx[place * c_tiles + t].reshape(c_out.shape[1:])

    for load in loads[7:]:
        load.wait()

    def parent_solver(b, lb, after, far):
        for d in range(1, rows):
            q = lax.rem(row + d, rows)
            arrived = zf.at[q, lb]
            pltpu.make_async_copy(arrived, arrived, zf_recv.at[q, lb]).wait()
        for g in range(p_group):
            total = side[lb * p_group + g]
            for d in range(1, rows):
                total = total - zf[lax.rem(row + d, rows), lb, g].astype(F32)
            side[lb * p_group + g] = total
        solve(b, lb, p_group, px, lambda n: side[n], lambda k: p_slots[k], p_ranks, v_pr, v_pl,
              ps, pf, pf_send, pf_recv, v_pinv, v_ir, v_il, in_ranks, after, far)

    front(p_blocks * rows, p_blocks, p_group, row,
          lambda d: lax.rem(row + d, rows), lambda d: row + d < rows,
          px, pz_send, pz_recv, px_send, px_recv, parent_solver)

    for q in range(rows):
        @pl.when(row != q)
        def _():
            for l in range(p_blocks):
                lifted(q, l).wait_send()

    for t in range(p_tiles):
        p_out[t] = px[row * p_tiles + t].reshape(p_out.shape[1:])


def on_device(
    rows,
    cols,
    parent_rhs, parent_inverse, parent_left, parent_right, parent_ranks, parent_slots,
    inner_left, inner_right, inner_ranks,
    child_rhs, child_inverse, child_left, child_right, child_ranks, child_slots,
    child_inner_left, child_inner_right, child_inner_ranks,
    border_left, border_right, border_ranks, border_map,
):
    tile = parent_inverse.shape[1]
    nrhs = parent_rhs.shape[1]
    width = nrhs // cols
    p_tiles, c_tiles = parent_inverse.shape[0], child_inverse.shape[0]
    p_blocks, c_blocks = inner_left.shape[0], child_inner_left.shape[0]
    p_group, c_group = p_tiles // p_blocks, c_tiles // c_blocks
    n_border = border_left.shape[0]
    p_all = p_tiles * rows
    c_all = c_tiles * (rows // 2)

    index = jnp.arange(n_border, dtype=jnp.int32)[:, None]
    hit = border_map[:, None] == jnp.arange(p_all, dtype=jnp.int32)[None, :]
    inverse_map = jnp.min(jnp.where(hit, index, n_border), axis=0)

    numbers = (
        parent_ranks, parent_slots, inner_ranks, child_ranks, child_slots,
        child_inner_ranks, border_ranks, inverse_map,
    )
    big = (
        parent_inverse, parent_left, parent_right, inner_left, inner_right,
        child_inverse, child_left, child_right, child_inner_left, child_inner_right,
        border_left, border_right,
    )
    smem = pl.BlockSpec(memory_space=pltpu.SMEM)
    vmem = pl.BlockSpec(memory_space=pltpu.VMEM)
    hbm = pl.BlockSpec(memory_space=pl.ANY)
    dma = pltpu.SemaphoreType.DMA
    c_out, p_out = pl.pallas_call(
        functools.partial(kernel, rows, cols, tuple(a.shape for a in numbers)),
        out_shape=(
            jax.ShapeDtypeStruct((c_tiles, nrhs, tile), BF16),
            jax.ShapeDtypeStruct((p_tiles, nrhs, tile), BF16),
        ),
        in_specs=[smem] + [vmem] * 2 + [hbm] * len(big),
        out_specs=(vmem, vmem),
        scratch_shapes=[pltpu.VMEM(a.shape, a.dtype) for a in big]
        + [
            pltpu.VMEM((c_all, cols, width, tile), BF16),
            pltpu.VMEM((p_all, cols, width, tile), BF16),
            pltpu.VMEM((c_blocks, cols, c_group, width, tile), BF16),
            pltpu.VMEM((c_blocks, cols, c_group, width, tile), BF16),
            pltpu.VMEM((p_blocks, cols, p_group, width, tile), BF16),
            pltpu.VMEM((p_blocks, cols, p_group, width, tile), BF16),
            pltpu.VMEM((cols, n_border, width, tile), BF16),
            pltpu.VMEM((cols, n_border, width, tile), BF16),
            pltpu.VMEM((n_border + 1, width, tile), F32),
            pltpu.VMEM((rows, p_blocks, p_group, width, tile), BF16),
            pltpu.VMEM((rows, p_blocks, p_group, width, tile), BF16),
            pltpu.VMEM((p_tiles, width, tile), F32),
            pltpu.VMEM((max(parent_left.shape[1], child_left.shape[1]), nrhs, tile), BF16),
            pltpu.VMEM((p_tiles, cols, width, tile), BF16),
            pltpu.VMEM((c_tiles, cols, width, tile), BF16),
            dma((len(big),)),
            dma((c_group, cols)), dma((c_blocks, c_group, cols)),
            dma((p_group, cols)), dma((p_blocks, p_group, cols)),
            dma((n_border, cols)), dma((n_border, cols)),
            dma((rows, p_blocks)), dma((rows, p_blocks)),
            dma((cols,)), dma((c_blocks * (rows // 2), cols)),
            dma((cols,)), dma((p_blocks * rows, cols)),
            dma((rows,)), dma((c_blocks * (rows // 2), c_group)),
            dma((rows,)), dma((p_blocks * rows, p_group)),
        ],
        compiler_params=pltpu.CompilerParams(
            collective_id=0, has_side_effects=True, vmem_limit_bytes=60 * 1024 * 1024
        ),
    )(
        jnp.concatenate([a.reshape(-1) for a in numbers]),
        parent_rhs, child_rhs,
        *big,
    )
    return (
        c_out.transpose(0, 2, 1).reshape(c_tiles * tile, nrhs),
        p_out.transpose(0, 2, 1).reshape(p_tiles * tile, nrhs),
    )


def solution(mesh):
    two, three, four = P("row", None), P("row", None, None), P("row", None, None, None)
    placed = (
        two, three, P("row", "col", None, None), P("row", "col", None, None),
        P("row", "col"), P("col"), four, four, two,
        two, three, P("row", "col", None, None), P("row", "col", None, None),
        P("row", "col"), P(None, "col"), four, four, two,
        P("row", "col", None, None), P("row", "col", None, None), P("row", "col"), P("row"),
    )
    return jax.shard_map(
        functools.partial(on_device, mesh.shape["row"], mesh.shape["col"]),
        mesh=mesh,
        in_specs=placed,
        out_specs=(two, two),
        check_vma=False,
    )
```
